32 devices in a mesh: groups: 2 (over x), gy: 16 (over z, y, core).
Axes of the slice: x: 2, y: 2, z: 4, core: 2. Of those that a mesh axis runs over, the one named last changes fastest.
Arguments:
- observed: float32 [2048, 16, 256], P(('groups', 'gy')), parts along dimension 0, may hold values from -6 to 6
- tf_table: float32 [16], replicated, may hold values from 0.2 to 2
- tilt_index: int32 [513, 129], replicated, may hold values from 0 to 15
- wedge: int32 [513, 129], replicated, may hold values 0 or 1
Outputs:
- restored: float32 [2048, 16, 256], P(('groups', 'gy')), parts along dimension 0
The draws below stay inside these ranges and needn't reach their ends.
There are 2 independent parts, one for each index of `groups`. The reference program is written for one: setup_inputs(seed, part) draws one part's arguments, and reference() takes and returns one part's arrays. A program takes and returns all parts, laid end to end along the dimension named above; an argument that names none is the same for every part. Nothing has to cross between parts.
All inputs are finite; a program needn't handle non-finite values.
Results may differ from the reference program's by a relative error of at most 0.00011.
Values sent between devices are 32-bit elements; how exact they have to be, the bound alone decides.
A program may use at most 64 MiB of HBM per device.

```python
import math
import jax
import jax.numpy as jnp
from jax import lax

NX = 1024
NZ = 256
LEVELS = 16
OUTER = 2
PASSES = 2
NY = 16
NXH = 513
NZH = 129


def with_ends(values, own_key, smallest, top_value):
    shape = values.shape
    place = [jax.random.randint(jax.random.fold_in(own_key, axis), (), 0, shape[axis]) for axis in range(len(shape))]
    values = values.at[tuple(place)].set(smallest)
    longest = shape.index(max(shape))
    place[longest] = (place[longest] + 1) % shape[longest]
    return values.at[tuple(place)].set(top_value)


def block_levels(key, extent, cuts, least, top_value):
    loudness, own = 1.0, jax.random.fold_in(key, 6)
    for dim, shards_of in cuts:
        draws = jnp.exp(jax.random.uniform(jax.random.fold_in(own, dim), (shards_of,), jnp.float32, least / len(cuts), top_value / len(cuts)))
        loudness = loudness * jnp.repeat(draws, extent[dim] // shards_of).reshape([-1 if axis == dim else 1 for axis in range(len(extent))])
    return loudness


def bell_draw(own_key, extent, scale, reach, cuts=(), kind=jnp.bfloat16):
    level = block_levels(own_key, extent, cuts, -0.22, 0.18) if cuts else 1.0
    array = jax.random.normal(own_key, extent, jnp.float32) * scale * level
    return jnp.minimum(jnp.maximum(array, -reach), reach).astype(kind)


def setup_inputs(seed: int = 0, part: int = 0) -> dict:
    splits = jax.random.split(jax.random.key(seed), 5)
    part_keys = jax.random.split(jax.random.fold_in(splits[4], part), 5)
    return {
        "observed": bell_draw(part_keys[0], (NX, NY, NZ), 1.0, 6.0, ((0, 16),), jnp.float32),
        "tf_table": jnp.clip(jnp.exp(jax.random.uniform(splits[1], (LEVELS,), jnp.float32, math.log(0.2), math.log(2.0))), 0.2, 2.0),
        "tilt_index": with_ends(jax.random.randint(splits[2], (NXH, NZH), 0, LEVELS), jax.random.fold_in(splits[2], 1), 0, LEVELS - 1).astype(jnp.int32),
        "wedge": with_ends((jax.random.randint(splits[3], (NXH, NZH), 0, 4) < 3).astype(jnp.int32), jax.random.fold_in(splits[3], 1), 0, 1),
    }


step_dual = 0.14
step_primal = 0.14
huber_eps = 0.05
bound_dual = 0.5

def curvature(field, axis):
    widths = [(0, 0), (0, 0), (0, 0)]
    widths[axis] = (1, 1)
    padded = jnp.pad(field, widths)
    upper = lax.slice_in_dim(padded, 2, padded.shape[axis], axis=axis)
    lower = lax.slice_in_dim(padded, 0, padded.shape[axis] - 2, axis=axis)
    return upper + lower - 2.0 * field

def denoise(target, duals):
    field = target
    lead = target
    for sweep in range(PASSES):
        raised = [(duals[axis] + step_dual * curvature(lead, axis)) / (1.0 + step_dual * huber_eps / bound_dual) for axis in range(3)]
        total = raised[0] * raised[0] + raised[1] * raised[1] + raised[2] * raised[2]
        shrink = jnp.sqrt(jnp.maximum(1.0, total / (bound_dual * bound_dual)))
        duals = (raised[0] / shrink, raised[1] / shrink, raised[2] / shrink)
        adjoint = curvature(duals[0], 0) + curvature(duals[1], 1) + curvature(duals[2], 2)
        updated = (field - step_primal * adjoint + step_primal * target) / (1.0 + step_primal)
        lead = 2.0 * updated - field
        field = updated
    return (field, duals)

def reference(observed, tf_table, tilt_index, wedge):
    half_rows = tf_table[tilt_index] * wedge.astype(tf_table.dtype)
    response = jnp.concatenate([half_rows, half_rows[NX // 2 - 1:0:-1]], 0)
    denom = response * response + 1.0
    g_data = (response / denom)[:, None, :]
    g_prior = (1.0 / denom)[:, None, :]
    spectrum = jnp.fft.rfft2(observed, axes=(0, 2))
    current = observed
    duals = (jnp.zeros_like(observed), jnp.zeros_like(observed), jnp.zeros_like(observed))
    for outer in range(OUTER):
        mixed = g_data * spectrum + g_prior * jnp.fft.rfft2(current, axes=(0, 2))
        target = jnp.fft.irfft2(mixed, s=(NX, NZ), axes=(0, 2)).astype(observed.dtype)
        current, duals = denoise(target, duals)
    return current
```

```python
import functools
import math

import jax
import jax.numpy as jnp
import numpy as np
from jax import lax
from jax.experimental import pallas as pl
from jax.experimental.pallas import tpu as pltpu
from jax.sharding import PartitionSpec as P

OUTER = 2
PASSES = 2
HALO = 8

step_dual = 0.14
step_primal = 0.14
huber_eps = 0.05
bound_dual = 0.5
MESH = pl.DeviceIdType.MESH
f32 = jnp.float32
bf16 = jnp.bfloat16


def split(value):
    high = value.astype(bf16)
    low = (value - high.astype(f32)).astype(bf16)
    return high, low


def dot3(a_high, a_low, b_high, b_low):
    dot = functools.partial(jnp.dot, preferred_element_type=f32)
    return dot(a_high, b_high) + (dot(a_high, b_low) + dot(a_low, b_high))


def kernel(
    n, chunks, part, block,
    cells_ref, table_ref, tilt_ref, wedge_ref, cos_ref, sin_ref, cas_ref, case_ref, zh_ref, zl_ref,
    out_ref,
    gathered, total, data_term, prior_gain, x_high, x_low, m_high, m_low, back,
    target, field, lead, dual_x, dual_y, dual_z, current, code,
    send_sem, recv_sem, back_send, back_recv, halo_send, halo_recv,
):
    me = lax.axis_index("gy")
    ny, rows, nz = cells_ref.shape
    nx = n * rows
    wide = rows + 2 * HALO
    half = n // 2
    row_blocks = nx // block
    chunk_rows = n * part

    barrier = pltpu.get_barrier_semaphore()

    def greet(o, carry):
        pl.semaphore_signal(
            barrier, inc=1, device_id={"gy": lax.rem(me + o, n)}, device_id_type=MESH
        )
        return carry

    lax.fori_loop(1, n, greet, 0)
    pl.semaphore_wait(barrier, n - 1)

    def far(k):
        return (1 - me // half) * half + lax.rem(me + k, half)

    def near(k):
        return (me // half) * half + lax.rem(me + k, half)

    def each_peer(action):
        def first(k, carry):
            action(far(k))
            return carry

        def second(k, carry):
            action(near(k))
            return carry

        lax.fori_loop(0, half, first, 0)
        lax.fori_loop(1, half, second, 0)

    def forward_copy(source, c, peer, owner):
        return pltpu.make_async_remote_copy(
            src_ref=source.at[peer, pl.ds(c * part, part), :],
            dst_ref=gathered.at[c, pl.ds(pl.multiple_of(owner * part, part), part), :],
            send_sem=send_sem.at[c, peer],
            recv_sem=recv_sem.at[c, owner],
            device_id={"gy": peer},
            device_id_type=MESH,
        )

    def back_copy(c, peer, owner):
        return pltpu.make_async_remote_copy(
            src_ref=back.at[c, pl.ds(pl.multiple_of(peer * part, part), part), :],
            dst_ref=target.at[owner, pl.ds(HALO + c * part, part), :],
            send_sem=back_send.at[c, peer],
            recv_sem=back_recv.at[c, owner],
            device_id={"gy": peer},
            device_id_type=MESH,
        )

    def send_forward(source):
        for c in range(chunks):
            each_peer(lambda peer: forward_copy(source, c, peer, me).start())
            gathered[c, pl.ds(pl.multiple_of(me * part, part), part), :] = source[
                me, pl.ds(c * part, part), :
            ]

    def make_tables():
        def group(m, carry):
            lines = (
                cos_ref[pl.ds(m, 1), :] * cas_ref[...] + sin_ref[pl.ds(m, 1), :] * case_ref[...]
            )
            high, low = split(lines)
            at = pl.ds(pl.multiple_of(m * part, part), part)
            x_high[at, :] = high
            x_low[at, :] = low
            return carry

        lax.fori_loop(0, nx // part, group, 0)

    def make_filter():
        lines, columns = tilt_ref.shape
        code[...] = jnp.zeros_like(code)
        code[0:lines, 0:columns] = jnp.where(wedge_ref[...] == 0, 0, tilt_ref[...] + 1).astype(f32)
        depth, width = code.shape
        kz = lax.broadcasted_iota(jnp.int32, (width, nz), 1)
        pick_z = jnp.where(
            lax.broadcasted_iota(jnp.int32, (width, nz), 0) == jnp.minimum(kz, nz - kz), 1.0, 0.0
        ).astype(bf16)
        spread = jnp.dot(code[...].astype(bf16), pick_z, preferred_element_type=f32).astype(bf16)

        def body(b, carry):
            line = b * block + lax.broadcasted_iota(jnp.int32, (block, depth), 0)
            c = line // chunk_rows
            owner = (line % chunk_rows) // part
            kx = owner * rows + c * part + line % part
            column = lax.broadcasted_iota(jnp.int32, (block, depth), 1)
            pick_x = jnp.where(column == jnp.minimum(kx, nx - kx), 1.0, 0.0).astype(bf16)
            which = jnp.dot(pick_x, spread, preferred_element_type=f32)
            response = jnp.zeros_like(which)
            for level in range(table_ref.shape[0]):
                response = jnp.where(which == level + 1.0, table_ref[level], response)
            prior = 1.0 / (response * response + 1.0)
            at = pl.ds(pl.multiple_of(b * block, block), block)
            prior_gain[at, :] = prior
            data_term[at, :] = response * prior
            return carry

        lax.fori_loop(0, row_blocks, body, 0)

    def x_forward():
        for c in range(chunks):
            def arrived(o, carry):
                owner = lax.rem(me + o, n)
                forward_copy(current, c, owner, owner).wait_recv()
                return carry

            lax.fori_loop(1, n, arrived, 0)
            high, low = split(gathered[c])

            def body(b, carry):
                at = pl.ds(pl.multiple_of(b * block, block), block)
                span = pl.ds(c * chunk_rows, chunk_rows)
                product = dot3(x_high[at, span], x_low[at, span], high, low)
                if c == 0:
                    total[at, :] = product
                else:
                    total[at, :] += product
                return carry

            lax.fori_loop(0, row_blocks, body, 0)

    def mix(outer):
        def body(b, carry):
            at = pl.ds(pl.multiple_of(b * block, block), block)
            high, low = split(total[at, :])
            spectrum = dot3(high, low, zh_ref[...], zl_ref[...])
            if outer == 0:
                data_term[at, :] = data_term[at, :] * spectrum
            mixed = data_term[at, :] + prior_gain[at, :] * spectrum
            high, low = split(mixed)
            high, low = split(dot3(high, low, zh_ref[...], zl_ref[...]))
            m_high[at, :] = high
            m_low[at, :] = low
            return carry

        lax.fori_loop(0, row_blocks, body, 0)

    order = [0] + ([chunks - 1] if chunks > 1 else []) + list(range(1, chunks - 1))
    before, after = lax.rem(me + n - 1, n), lax.rem(me + 1, n)

    def halo_up():
        return pltpu.make_async_remote_copy(
            src_ref=target.at[:, pl.ds(rows, HALO), :],
            dst_ref=target.at[:, pl.ds(0, HALO), :],
            send_sem=halo_send.at[0],
            recv_sem=halo_recv.at[0],
            device_id={"gy": after},
            device_id_type=MESH,
        )

    def halo_down():
        return pltpu.make_async_remote_copy(
            src_ref=target.at[:, pl.ds(HALO, HALO), :],
            dst_ref=target.at[:, pl.ds(HALO + rows, HALO), :],
            send_sem=halo_send.at[1],
            recv_sem=halo_recv.at[1],
            device_id={"gy": before},
            device_id_type=MESH,
        )

    def x_backward():
        for c in order:
            span = pl.ds(c * chunk_rows, chunk_rows)
            step = min(block, chunk_rows)

            def body(b, carry):
                at = pl.ds(pl.multiple_of(b * step, step), step)
                line = pl.ds(pl.multiple_of(c * chunk_rows + b * step, step), step)
                back[c, at, :] = dot3(x_high[line, :], x_low[line, :], m_high[...], m_low[...])
                return carry

            lax.fori_loop(0, chunk_rows // step, body, 0)
            each_peer(lambda peer: back_copy(c, peer, me).start())
            target[me, pl.ds(HALO + c * part, part), :] = back[
                c, pl.ds(pl.multiple_of(me * part, part), part), :
            ]
        for c in order:
            def arrived(o, carry):
                owner = lax.rem(me + o, n)
                back_copy(c, owner, owner).wait_recv()
                return carry

            lax.fori_loop(1, n, arrived, 0)
            if c == order[0]:
                @pl.when(me > 0)
                def _():
                    halo_down().start()
            if c == chunks - 1:
                @pl.when(me < n - 1)
                def _():
                    halo_up().start()

        @pl.when(me > 0)
        def _():
            halo_up().wait_recv()
            halo_down().wait_send()

        @pl.when(me < n - 1)
        def _():
            halo_down().wait_recv()
            halo_up().wait_send()

        def sent(o, carry):
            for c in range(chunks):
                back_copy(c, lax.rem(me + o, n), me).wait_send()
            return carry

        lax.fori_loop(1, n, sent, 0)

    def wait_forward_sent(source):
        def sent(o, carry):
            for c in range(chunks):
                forward_copy(source, c, lax.rem(me + o, n), me).wait_send()
            return carry

        lax.fori_loop(1, n, sent, 0)

    def denoise(outer):
        column = lax.broadcasted_iota(jnp.int32, (wide, nz), 1)
        line = lax.broadcasted_iota(jnp.int32, (wide, nz), 0) + (me * rows - HALO)
        inside = jnp.where((line >= 0) & (line < nx), 1.0, 0.0)
        not_first = jnp.where(column > 0, 1.0, 0.0)
        not_last = jnp.where(column < nz - 1, 1.0, 0.0)

        def bend_x(value):
            return pltpu.roll(value, 1, 0) + pltpu.roll(value, wide - 1, 0) - 2.0 * value

        def bend_z(value):
            return (
                pltpu.roll(value, 1, 1) * not_first
                + pltpu.roll(value, nz - 1, 1) * not_last
                - 2.0 * value
            )

        def neighbours(ref, y):
            low = ref[jnp.maximum(y - 1, 0)] * jnp.where(y > 0, 1.0, 0.0)
            high = ref[jnp.minimum(y + 1, ny - 1)] * jnp.where(y < ny - 1, 1.0, 0.0)
            return low + high - 2.0 * ref[y]

        scale = 1.0 / (1.0 + step_dual * huber_eps / bound_dual)
        for sweep in range(PASSES):
            origin = target if sweep == 0 else lead
            base = target if sweep == 0 else field
            fresh = outer == 0 and sweep == 0

            def rise(y):
                here = origin[y]
                bends = (bend_x(here), neighbours(origin, y), bend_z(here))
                if fresh:
                    raised = [bend * (step_dual * scale) for bend in bends]
                else:
                    raised = [
                        dual[y] * scale + bend * (step_dual * scale)
                        for dual, bend in zip((dual_x, dual_y, dual_z), bends)
                    ]
                norm = raised[0] * raised[0] + raised[1] * raised[1] + raised[2] * raised[2]
                shrink = lax.rsqrt(jnp.maximum(1.0, norm * (1.0 / bound_dual**2))) * inside
                dual_x[y] = raised[0] * shrink
                dual_y[y] = raised[1] * shrink
                dual_z[y] = raised[2] * shrink

            def fall(y):
                adjoint = bend_x(dual_x[y]) + neighbours(dual_y, y) + bend_z(dual_z[y])
                old = base[y]
                updated = (
                    (old - step_primal * adjoint + step_primal * target[y])
                    * (1.0 / (1.0 + step_primal))
                    * inside
                )
                if sweep < PASSES - 1:
                    lead[y] = 2.0 * updated - old
                    field[y] = updated
                elif outer < OUTER - 1:
                    current[y] = updated[HALO : HALO + rows, :]
                else:
                    out_ref[y] = updated[HALO : HALO + rows, :]

            rise(0)

            def body(y, carry):
                rise(y)
                fall(y - 1)
                return carry

            lax.fori_loop(1, ny, body, 0)
            fall(ny - 1)

    send_forward(cells_ref)

    @pl.when(me == 0)
    def _():
        target[:, 0:HALO, :] = jnp.zeros((ny, HALO, nz), f32)

    @pl.when(me == n - 1)
    def _():
        target[:, rows + HALO : wide, :] = jnp.zeros((ny, HALO, nz), f32)

    make_tables()
    make_filter()
    for outer in range(OUTER):
        x_forward()
        mix(outer)
        wait_forward_sent(cells_ref if outer == 0 else current)
        x_backward()
        denoise(outer)
        if outer < OUTER - 1:
            send_forward(current)


def constants(n, rows, part, nz):
    nx = n * rows
    line = np.arange(nx)
    place = (line % (n * part)) // part * rows + line // (n * part) * part + line % part
    turn = 2.0 * math.pi / nx
    starts = place[::part]
    coarse = (starts[:, None] * place[None, :] % nx) * turn
    fine = (np.arange(part)[:, None] * place[None, :] % nx) * turn
    norm = 1.0 / math.sqrt(nx)
    tables = (
        np.cos(coarse),
        np.sin(coarse),
        (np.cos(fine) + np.sin(fine)) * norm,
        (np.cos(fine) - np.sin(fine)) * norm,
    )
    k = np.arange(nz)
    angle = (k[:, None] * k[None, :] % nz) * (2.0 * math.pi / nz)
    cas_z = ((np.cos(angle) + np.sin(angle)) / math.sqrt(nz)).astype(np.float32)
    z_high = cas_z.astype(bf16)
    z_low = (cas_z - z_high.astype(np.float32)).astype(bf16)
    return [jnp.asarray(t, f32) for t in tables] + [jnp.asarray(z_high), jnp.asarray(z_low)]


def local(n, observed, tf_table, tilt_index, wedge):
    rows, ny, nz = observed.shape
    nx = n * rows
    part = rows // 4 if rows % 32 == 0 else rows
    chunks = rows // part
    block = min(nx, 256)
    wide = rows + 2 * HALO
    lines, columns = tilt_index.shape
    depth, width = -(-lines // 128) * 128, -(-columns // 128) * 128
    tables = constants(n, rows, part, nz)
    vmem = pl.BlockSpec(memory_space=pltpu.VMEM)
    smem = pl.BlockSpec(memory_space=pltpu.SMEM)
    slab = pltpu.VMEM((ny, wide, nz), f32)
    plane = pltpu.VMEM((nx, nz), f32)
    result = pl.pallas_call(
        functools.partial(kernel, n, chunks, part, block),
        out_shape=jax.ShapeDtypeStruct((ny, rows, nz), f32),
        in_specs=[vmem, smem] + [vmem] * 8,
        out_specs=vmem,
        scratch_shapes=[
            pltpu.VMEM((chunks, n * part, nz), f32),
            plane,
            plane,
            plane,
            pltpu.VMEM((nx, nx), bf16),
            pltpu.VMEM((nx, nx), bf16),
            pltpu.VMEM((nx, nz), bf16),
            pltpu.VMEM((nx, nz), bf16),
            pltpu.VMEM((chunks, n * part, nz), f32),
            slab,
            slab,
            slab,
            slab,
            slab,
            slab,
            pltpu.VMEM((ny, rows, nz), f32),
            pltpu.VMEM((depth, width), f32),
            pltpu.SemaphoreType.DMA((chunks, n)),
            pltpu.SemaphoreType.DMA((chunks, n)),
            pltpu.SemaphoreType.DMA((chunks, n)),
            pltpu.SemaphoreType.DMA((chunks, n)),
            pltpu.SemaphoreType.DMA((2,)),
            pltpu.SemaphoreType.DMA((2,)),
        ],
        compiler_params=pltpu.CompilerParams(
            collective_id=0, has_side_effects=True, vmem_limit_bytes=60 * 1024 * 1024
        ),
    )(jnp.swapaxes(observed, 0, 1), tf_table, tilt_index, wedge, *tables)
    return jnp.swapaxes(result, 0, 1)


def solution(mesh):
    in_specs = (P(("groups", "gy"), None, None), P(), P(), P())
    out_specs = P(("groups", "gy"), None, None)
    body = functools.partial(local, mesh.shape["gy"])
    return jax.shard_map(body, mesh=mesh, in_specs=in_specs, out_specs=out_specs, check_vma=False)
```

```python
import functools
import math

import jax
import jax.numpy as jnp
import numpy as np
from jax import lax
from jax.experimental import pallas as pl
from jax.experimental.pallas import tpu as pltpu
from jax.sharding import PartitionSpec as P

OUTER = 2
PASSES = 2
GROUP = 8
LANES = 128

step_dual = 0.14
step_primal = 0.14
huber_eps = 0.05
bound_dual = 0.5
MESH = pl.DeviceIdType.MESH
f32 = jnp.float32
bf16 = jnp.bfloat16


def split(value):
    high = value.astype(bf16)
    low = (value - high.astype(f32)).astype(bf16)
    return high, low


def dot3(a_high, a_low, b_high, b_low):
    dot = functools.partial(jnp.dot, preferred_element_type=f32)
    return dot(a_high, b_high) + (dot(a_high, b_low) + dot(a_low, b_high))


def kernel(
    n, rows, order,
    cells_ref, table_ref, tilt_ref, wedge_ref, cos_ref, sin_ref, cas_ref, case_ref, zh_ref, zl_ref,
    out_ref,
    gathered, total, data_term, prior_gain, x_high, x_low, m_high, m_low, back,
    target, halo, field, lead, duals, current, code,
    send_sem, recv_sem, back_send, back_recv, halo_send, halo_recv,
):
    me = lax.axis_index("gy")
    chunks, slots = len(order), len(order[0])
    groups = chunks * slots
    seat = {g: (c, s) for c in range(chunks) for s, g in enumerate(order[c])}
    part = slots * GROUP
    ny, nz = out_ref.shape[0], out_ref.shape[2]
    nx = n * rows
    half = n // 2
    span_rows = n * part
    block = math.gcd(nx, 256)
    row_blocks = nx // block

    barrier = pltpu.get_barrier_semaphore()

    def greet(o, carry):
        pl.semaphore_signal(
            barrier, inc=1, device_id={"gy": lax.rem(me + o, n)}, device_id_type=MESH
        )
        return carry

    lax.fori_loop(1, n, greet, 0)

    def each_peer(action):
        def first(k, carry):
            action((1 - me // half) * half + lax.rem(me + k, half))
            return carry

        def second(k, carry):
            action((me // half) * half + lax.rem(me + k, half))
            return carry

        lax.fori_loop(0, half, first, 0)
        lax.fori_loop(1, half, second, 0)

    def every_other(action):
        def step(o, carry):
            action(lax.rem(me + o, n))
            return carry

        lax.fori_loop(1, n, step, 0)

    def forward_copy(c, peer, owner):
        return pltpu.make_async_remote_copy(
            src_ref=current.at[peer, c],
            dst_ref=gathered.at[c, owner],
            send_sem=send_sem.at[c, peer],
            recv_sem=recv_sem.at[c, owner],
            device_id={"gy": peer},
            device_id_type=MESH,
        )

    def back_copy(c, peer, owner):
        return pltpu.make_async_remote_copy(
            src_ref=back.at[c, peer],
            dst_ref=target.at[owner, c],
            send_sem=back_send.at[c, peer],
            recv_sem=back_recv.at[c, owner],
            device_id={"gy": peer},
            device_id_type=MESH,
        )

    def halo_copy(side):
        return pltpu.make_async_remote_copy(
            src_ref=target.at[:, 0, slots - 1 if side == 0 else 0],
            dst_ref=halo.at[side],
            send_sem=halo_send.at[side],
            recv_sem=halo_recv.at[side],
            device_id={"gy": lax.rem(me + (1 if side == 0 else n - 1), n)},
            device_id_type=MESH,
        )

    def send_forward(c):
        each_peer(lambda peer: forward_copy(c, peer, me).start())
        gathered[c, me] = current[me, c]

    def stage(y, carry):
        stride = ny * nz // LANES
        for z in range(nz // LANES):
            first = (y // GROUP * (nz // LANES) + z) * GROUP + y % GROUP
            lines = cells_ref[pl.ds(first, rows, stride=stride), :]
            for g, (c, s) in seat.items():
                current[y, c, s, :, z * LANES : (z + 1) * LANES] = lines[
                    g * GROUP : (g + 1) * GROUP, :
                ]
        return carry

    def make_tables():
        def body(m, carry):
            lines = jnp.concatenate(
                [
                    cos_ref[pl.ds(k, 1), :] * cas_ref[...] + sin_ref[pl.ds(k, 1), :] * case_ref[...]
                    for k in (2 * m, 2 * m + 1)
                ],
                axis=0,
            )
            at = pl.ds(pl.multiple_of(m * 2 * GROUP, 2 * GROUP), 2 * GROUP)
            x_high[at, :], x_low[at, :] = split(lines)
            return carry

        lax.fori_loop(0, nx // (2 * GROUP), body, 0)

    def make_filter():
        columns, lines = tilt_ref.shape
        code[...] = jnp.zeros_like(code)
        code[0:columns, 0:lines] = jnp.where(wedge_ref[...] == 0, 0, tilt_ref[...] + 1).astype(f32)
        width, depth = code.shape
        kz = lax.broadcasted_iota(jnp.int32, (nz, width), 0)
        pick_z = jnp.where(
            lax.broadcasted_iota(jnp.int32, (nz, width), 1) == jnp.minimum(kz, nz - kz), 1.0, 0.0
        ).astype(bf16)
        spread = jnp.dot(pick_z, code[...].astype(bf16), preferred_element_type=f32).astype(bf16)

        def body(b, carry):
            line = b * block + lax.broadcasted_iota(jnp.int32, (block, depth), 0)
            c = line // span_rows
            slot = line % part // GROUP
            group = slot if chunks == 1 else jnp.where(slot == 0, c, groups - 1 - c)
            kx = line % span_rows // part * rows + group * GROUP + line % GROUP
            column = lax.broadcasted_iota(jnp.int32, (block, depth), 1)
            pick_x = jnp.where(column == jnp.minimum(kx, nx - kx), 1.0, 0.0).astype(bf16)
            which = lax.dot_general(
                pick_x, spread, (((1,), (1,)), ((), ())), preferred_element_type=f32
            )
            response = jnp.zeros_like(which)
            for level in range(table_ref.shape[0]):
                response = jnp.where(which == level + 1.0, table_ref[level], response)
            prior = 1.0 / (response * response + 1.0)
            at = pl.ds(pl.multiple_of(b * block, block), block)
            prior_gain[at, :] = prior
            data_term[at, :] = response * prior
            return carry

        lax.fori_loop(0, row_blocks, body, 0)

    def filtered(outer):
        for c in range(chunks):
            every_other(lambda owner: forward_copy(c, owner, owner).wait_recv())
            high, low = split(gathered[c].reshape(span_rows, nz))
            high, low = split(dot3(high, low, zh_ref[...], zl_ref[...]))

            def body(b, carry):
                at = pl.ds(pl.multiple_of(b * block, block), block)
                span = pl.ds(c * span_rows, span_rows)
                spectrum = dot3(x_high[at, span], x_low[at, span], high, low)
                if c > 0:
                    spectrum = total[at, :] + spectrum
                if c < chunks - 1:
                    total[at, :] = spectrum
                    return carry
                if outer == 0:
                    data_term[at, :] = data_term[at, :] * spectrum
                a_high, a_low = split(data_term[at, :] + prior_gain[at, :] * spectrum)
                m_high[at, :], m_low[at, :] = split(dot3(a_high, a_low, zh_ref[...], zl_ref[...]))
                return carry

            lax.fori_loop(0, row_blocks, body, 0)

    def send_back(c):
        step = math.gcd(span_rows, 256)

        def body(b, carry):
            line = pl.ds(pl.multiple_of(c * span_rows + b * step, step), step)
            lines = dot3(x_high[line, :], x_low[line, :], m_high[...], m_low[...])
            count = step // part
            at = pl.ds(pl.multiple_of(b * count, count), count)
            back[c, at] = lines.reshape(count, slots, GROUP, nz)
            return carry

        lax.fori_loop(0, span_rows // step, body, 0)
        each_peer(lambda peer: back_copy(c, peer, me).start())
        target[me, c] = back[c, me]

    def denoise(outer, index, low, high):
        dual_x, dual_y, dual_z = duals[3 * index : 3 * index + 3]
        wide = (high - low + 2) * GROUP
        column = lax.broadcasted_iota(jnp.int32, (wide, nz), 1)
        not_first = jnp.where(column > 0, 1.0, 0.0)
        not_last = jnp.where(column < nz - 1, 1.0, 0.0)
        edge = low == 0 or high == groups
        if edge:
            line = lax.broadcasted_iota(jnp.int32, (wide, nz), 0) + (me * rows + (low - 1) * GROUP)
            inside = jnp.where((line >= 0) & (line < nx), 1.0, 0.0)

        def bend_x(value):
            return pltpu.roll(value, 1, 0) + pltpu.roll(value, wide - 1, 0) - 2.0 * value

        def bend_z(value):
            return (
                pltpu.roll(value, 1, 1) * not_first
                + pltpu.roll(value, nz - 1, 1) * not_last
                - 2.0 * value
            )

        def neighbours(get, y):
            below = get(jnp.maximum(y - 1, 0)) * jnp.where(y > 0, 1.0, 0.0)
            above = get(jnp.minimum(y + 1, ny - 1)) * jnp.where(y < ny - 1, 1.0, 0.0)
            return below + above - 2.0 * get(y)

        def goal(y):
            pieces = []
            for g in range(low - 1, high + 1):
                if g < 0:
                    pieces.append(halo[0, y])
                elif g >= groups:
                    pieces.append(halo[1, y])
                else:
                    pieces.append(target[y, seat[g][0], seat[g][1]])
            return jnp.concatenate(pieces, axis=0)

        def reader(ref):
            return lambda y: ref[y, 0:wide, :]

        scale = 1.0 / (1.0 + step_dual * huber_eps / bound_dual)
        for sweep in range(PASSES):
            origin = goal if sweep == 0 else reader(lead)
            base = goal if sweep == 0 else reader(field)
            fresh = outer == 0 and sweep == 0

            def rise(y):
                here = origin(y)
                bends = (bend_x(here), neighbours(origin, y), bend_z(here))
                if fresh:
                    raised = [bend * (step_dual * scale) for bend in bends]
                else:
                    raised = [
                        dual[y] * scale + bend * (step_dual * scale)
                        for dual, bend in zip((dual_x, dual_y, dual_z), bends)
                    ]
                norm = raised[0] * raised[0] + raised[1] * raised[1] + raised[2] * raised[2]
                shrink = lax.rsqrt(jnp.maximum(1.0, norm * (1.0 / bound_dual**2)))
                if edge:
                    shrink = shrink * inside
                dual_x[y] = raised[0] * shrink
                dual_y[y] = raised[1] * shrink
                dual_z[y] = raised[2] * shrink

            def fall(y):
                adjoint = (
                    bend_x(dual_x[y]) + neighbours(lambda at: dual_y[at], y) + bend_z(dual_z[y])
                )
                old = base(y)
                updated = (old - step_primal * adjoint + step_primal * goal(y)) * (
                    1.0 / (1.0 + step_primal)
                )
                if sweep < PASSES - 1:
                    if edge:
                        updated = updated * inside
                    lead[y, 0:wide, :] = 2.0 * updated - old
                    field[y, 0:wide, :] = updated
                elif outer < OUTER - 1:
                    for g in range(low, high):
                        start = (g - low + 1) * GROUP
                        current[y, seat[g][0], seat[g][1]] = updated[start : start + GROUP, :]
                else:
                    out_ref[y, low * GROUP : high * GROUP, :] = updated[GROUP : wide - GROUP, :]

            rise(0)

            def body(y, carry):
                rise(y)
                fall(y - 1)
                return carry

            lax.fori_loop(1, ny, body, 0)
            fall(ny - 1)

    lax.fori_loop(0, ny, stage, 0)
    pl.semaphore_wait(barrier, n - 1)
    for c in range(chunks):
        send_forward(c)

    @pl.when(me == 0)
    def _():
        halo[0] = jnp.zeros(halo.shape[1:], f32)

    @pl.when(me == n - 1)
    def _():
        halo[1] = jnp.zeros(halo.shape[1:], f32)

    make_tables()
    make_filter()
    quarter = groups // 4
    for outer in range(OUTER):
        filtered(outer)
        for c in range(chunks):
            every_other(lambda peer: forward_copy(c, peer, me).wait_send())
        for c in range(chunks):
            send_back(c)

        def arrive(some):
            for c in some:
                every_other(lambda owner: back_copy(c, owner, owner).wait_recv())

        arrive([0])

        @pl.when(me < n - 1)
        def _():
            halo_copy(0).start()

        @pl.when(me > 0)
        def _():
            halo_copy(1).start()

        early = list(range(1, quarter + 1)) if chunks > 1 else []
        arrive(early)

        @pl.when(me > 0)
        def _():
            halo_copy(0).wait_recv()

        @pl.when(me < n - 1)
        def _():
            halo_copy(1).wait_recv()

        done = 0
        if chunks > 1:
            denoise(outer, 0, 0, quarter)
            denoise(outer, 1, groups - quarter, groups)
            done = quarter
            if outer < OUTER - 1:
                for c in range(done):
                    send_forward(c)
            arrive(range(quarter + 1, chunks))
            denoise(outer, 2, quarter, groups - quarter)
        else:
            denoise(outer, 0, 0, groups)

        @pl.when(me < n - 1)
        def _():
            halo_copy(0).wait_send()

        @pl.when(me > 0)
        def _():
            halo_copy(1).wait_send()

        for c in range(chunks):
            every_other(lambda peer: back_copy(c, peer, me).wait_send())
        if outer < OUTER - 1:
            for c in range(done, chunks):
                send_forward(c)


def constants(n, rows, order, nz):
    nx = n * rows
    place = np.array(
        [
            d * rows + g * GROUP + r
            for some in order
            for d in range(n)
            for g in some
            for r in range(GROUP)
        ]
    )
    turn = 2.0 * math.pi / nx
    coarse = (place[::GROUP, None] * place[None, :] % nx) * turn
    fine = (np.arange(GROUP)[:, None] * place[None, :] % nx) * turn
    norm = 1.0 / math.sqrt(nx)
    tables = (
        np.cos(coarse),
        np.sin(coarse),
        (np.cos(fine) + np.sin(fine)) * norm,
        (np.cos(fine) - np.sin(fine)) * norm,
    )
    k = np.arange(nz)
    angle = (k[:, None] * k[None, :] % nz) * (2.0 * math.pi / nz)
    cas_z = ((np.cos(angle) + np.sin(angle)) / math.sqrt(nz)).astype(np.float32)
    z_high = cas_z.astype(bf16)
    z_low = (cas_z - z_high.astype(np.float32)).astype(bf16)
    return [jnp.asarray(t, f32) for t in tables] + [jnp.asarray(z_high), jnp.asarray(z_low)]


def local(n, observed, tf_table, tilt_index, wedge):
    rows, ny, nz = observed.shape
    nx = n * rows
    groups = rows // GROUP
    if groups % 4 == 0:
        order = [(c, groups - 1 - c) for c in range(groups // 2)]
        sizes = [groups // 4, groups // 4, groups // 2]
    else:
        order = [tuple(range(groups))]
        sizes = [groups]
    chunks, slots = len(order), len(order[0])
    lines, columns = tilt_index.shape
    depth, width = -(-lines // 128) * 128, -(-columns // 128) * 128
    tables = constants(n, rows, order, nz)
    tiles = observed.reshape(rows, ny // GROUP, GROUP, nz // LANES, LANES)
    tiles = tiles.transpose(0, 1, 3, 2, 4).reshape(-1, LANES)
    vmem = pl.BlockSpec(memory_space=pltpu.VMEM)
    smem = pl.BlockSpec(memory_space=pltpu.SMEM)
    tile_rows = [(size + 2) * GROUP for size in sizes]
    scratch_tile = pltpu.VMEM((ny, max(tile_rows), nz), f32)
    plane = pltpu.VMEM((nx, nz), f32)
    blocks = pltpu.VMEM((chunks, n, slots, GROUP, nz), f32)
    cells = pltpu.VMEM((ny, chunks, slots, GROUP, nz), f32)
    semaphores = pltpu.SemaphoreType.DMA((chunks, n))
    result = pl.pallas_call(
        functools.partial(kernel, n, rows, order),
        out_shape=jax.ShapeDtypeStruct((ny, rows, nz), f32),
        in_specs=[vmem, smem] + [vmem] * 8,
        out_specs=vmem,
        scratch_shapes=[
            blocks,
            plane,
            plane,
            plane,
            pltpu.VMEM((nx, nx), bf16),
            pltpu.VMEM((nx, nx), bf16),
            pltpu.VMEM((nx, nz), bf16),
            pltpu.VMEM((nx, nz), bf16),
            blocks,
            cells,
            pltpu.VMEM((2, ny, GROUP, nz), f32),
            scratch_tile,
            scratch_tile,
            [pltpu.VMEM((ny, size, nz), f32) for size in tile_rows for _ in range(3)],
            cells,
            pltpu.VMEM((width, depth), f32),
            semaphores,
            semaphores,
            semaphores,
            semaphores,
            pltpu.SemaphoreType.DMA((2,)),
            pltpu.SemaphoreType.DMA((2,)),
        ],
        compiler_params=pltpu.CompilerParams(
            collective_id=0, has_side_effects=True, vmem_limit_bytes=60 * 1024 * 1024
        ),
    )(tiles, tf_table, tilt_index.T, wedge.T, *tables)
    return jnp.swapaxes(result, 0, 1)


def solution(mesh):
    in_specs = (P(("groups", "gy"), None, None), P(), P(), P())
    out_specs = P(("groups", "gy"), None, None)
    body = functools.partial(local, mesh.shape["gy"])
    return jax.shard_map(body, mesh=mesh, in_specs=in_specs, out_specs=out_specs, check_vma=False)
```

```python
import functools
import math

import jax
import jax.numpy as jnp
import numpy as np
from jax import lax
from jax.experimental import pallas as pl
from jax.experimental.pallas import tpu as pltpu
from jax.sharding import PartitionSpec as P

OUTER = 2
PASSES = 2
GROUP = 8
LANES = 128

step_dual = 0.14
step_primal = 0.14
huber_eps = 0.05
bound_dual = 0.5
relax = 1.0 / (1.0 + step_dual * huber_eps / bound_dual)
gain = step_dual * relax
MESH = pl.DeviceIdType.MESH
f32 = jnp.float32
bf16 = jnp.bfloat16


def split(value):
    high = value.astype(bf16)
    low = (value - high.astype(f32)).astype(bf16)
    return high, low


def dot3(a_high, a_low, b_high, b_low):
    dot = functools.partial(jnp.dot, preferred_element_type=f32)
    return dot(a_high, b_high) + (dot(a_high, b_low) + dot(a_low, b_high))


def kernel(
    n, rows, order,
    cells_ref, table_ref, tilt_ref, wedge_ref, cos_ref, sin_ref, cas_ref, case_ref, zh_ref, zl_ref,
    out_ref,
    gathered, total, data_term, prior_gain, x_high, x_low, m_high, m_low, back,
    target, halo, goal, field, lead, duals, current, code,
    send_sem, recv_sem, back_send, back_recv, halo_send, halo_recv,
):
    me = lax.axis_index("gy")
    chunks, slots = len(order), len(order[0])
    groups = chunks * slots
    seat = {g: (c, s) for c in range(chunks) for s, g in enumerate(order[c])}
    part = slots * GROUP
    ny, nz = out_ref.shape[0], out_ref.shape[2]
    nx = n * rows
    half = n // 2
    span_rows = n * part
    block = math.gcd(nx, 256)
    row_blocks = nx // block

    barrier = pltpu.get_barrier_semaphore()

    def greet(o, carry):
        pl.semaphore_signal(
            barrier, inc=1, device_id={"gy": lax.rem(me + o, n)}, device_id_type=MESH
        )
        return carry

    lax.fori_loop(1, n, greet, 0)

    def each_peer(action):
        def first(k, carry):
            action((1 - me // half) * half + lax.rem(me + k, half))
            return carry

        def second(k, carry):
            action((me // half) * half + lax.rem(me + k, half))
            return carry

        lax.fori_loop(0, half, first, 0)
        lax.fori_loop(1, half, second, 0)

    def every_other(action):
        def step(o, carry):
            action(lax.rem(me + o, n))
            return carry

        lax.fori_loop(1, n, step, 0)

    def forward_copy(c, peer, owner):
        return pltpu.make_async_remote_copy(
            src_ref=current.at[peer, c],
            dst_ref=gathered.at[c, owner],
            send_sem=send_sem.at[c, peer],
            recv_sem=recv_sem.at[c, owner],
            device_id={"gy": peer},
            device_id_type=MESH,
        )

    def back_copy(c, peer, owner):
        return pltpu.make_async_remote_copy(
            src_ref=back.at[c, peer],
            dst_ref=target.at[owner, c],
            send_sem=back_send.at[c, peer],
            recv_sem=back_recv.at[c, owner],
            device_id={"gy": peer},
            device_id_type=MESH,
        )

    def halo_copy(side):
        return pltpu.make_async_remote_copy(
            src_ref=target.at[:, 0, slots - 1 if side == 0 else 0],
            dst_ref=halo.at[side],
            send_sem=halo_send.at[side],
            recv_sem=halo_recv.at[side],
            device_id={"gy": lax.rem(me + (1 if side == 0 else n - 1), n)},
            device_id_type=MESH,
        )

    def send_forward(c):
        each_peer(lambda peer: forward_copy(c, peer, me).start())
        gathered[c, me] = current[me, c]

    def stage(y, carry):
        stride = ny * nz // LANES
        for z in range(nz // LANES):
            first = (y // GROUP * (nz // LANES) + z) * GROUP + y % GROUP
            lines = cells_ref[pl.ds(first, rows, stride=stride), :]
            for g, (c, s) in seat.items():
                current[y, c, s, :, z * LANES : (z + 1) * LANES] = lines[
                    g * GROUP : (g + 1) * GROUP, :
                ]
        return carry

    def make_tables():
        def body(m, carry):
            lines = jnp.concatenate(
                [
                    cos_ref[pl.ds(k, 1), :] * cas_ref[...] + sin_ref[pl.ds(k, 1), :] * case_ref[...]
                    for k in (2 * m, 2 * m + 1)
                ],
                axis=0,
            )
            at = pl.ds(pl.multiple_of(m * 2 * GROUP, 2 * GROUP), 2 * GROUP)
            x_high[at, :], x_low[at, :] = split(lines)
            return carry

        lax.fori_loop(0, nx // (2 * GROUP), body, 0)

    def make_filter():
        columns, lines = tilt_ref.shape
        code[...] = jnp.zeros_like(code)
        code[0:columns, 0:lines] = jnp.where(wedge_ref[...] == 0, 0, tilt_ref[...] + 1).astype(f32)
        width, depth = code.shape
        kz = lax.broadcasted_iota(jnp.int32, (nz, width), 0)
        pick_z = jnp.where(
            lax.broadcasted_iota(jnp.int32, (nz, width), 1) == jnp.minimum(kz, nz - kz), 1.0, 0.0
        ).astype(bf16)
        spread = jnp.dot(pick_z, code[...].astype(bf16), preferred_element_type=f32).astype(bf16)

        def body(b, carry):
            line = b * block + lax.broadcasted_iota(jnp.int32, (block, depth), 0)
            c = line // span_rows
            slot = line % part // GROUP
            group = slot if chunks == 1 else jnp.where(slot == 0, c, groups - 1 - c)
            kx = line % span_rows // part * rows + group * GROUP + line % GROUP
            column = lax.broadcasted_iota(jnp.int32, (block, depth), 1)
            pick_x = jnp.where(column == jnp.minimum(kx, nx - kx), 1.0, 0.0).astype(bf16)
            which = lax.dot_general(
                pick_x, spread, (((1,), (1,)), ((), ())), preferred_element_type=f32
            )
            response = jnp.zeros_like(which)
            for level in range(table_ref.shape[0]):
                response = jnp.where(which == level + 1.0, table_ref[level], response)
            prior = 1.0 / (response * response + 1.0)
            at = pl.ds(pl.multiple_of(b * block, block), block)
            prior_gain[at, :] = prior
            data_term[at, :] = response * prior
            return carry

        lax.fori_loop(0, row_blocks, body, 0)

    def filtered(outer):
        for c in range(chunks):
            every_other(lambda owner: forward_copy(c, owner, owner).wait_recv())
            high, low = split(gathered[c].reshape(span_rows, nz))
            high, low = split(dot3(high, low, zh_ref[...], zl_ref[...]))

            def body(b, carry):
                at = pl.ds(pl.multiple_of(b * block, block), block)
                span = pl.ds(c * span_rows, span_rows)
                spectrum = dot3(x_high[at, span], x_low[at, span], high, low)
                if c > 0:
                    spectrum = total[at, :] + spectrum
                if c < chunks - 1:
                    total[at, :] = spectrum
                    return carry
                if outer == 0:
                    spectrum = spectrum * gain
                    data_term[at, :] = data_term[at, :] * spectrum
                a_high, a_low = split(data_term[at, :] + prior_gain[at, :] * spectrum)
                m_high[at, :], m_low[at, :] = split(dot3(a_high, a_low, zh_ref[...], zl_ref[...]))
                return carry

            lax.fori_loop(0, row_blocks, body, 0)

    def send_back(c):
        step = math.gcd(span_rows, 256)

        def body(b, carry):
            line = pl.ds(pl.multiple_of(c * span_rows + b * step, step), step)
            lines = dot3(x_high[line, :], x_low[line, :], m_high[...], m_low[...])
            count = step // part
            at = pl.ds(pl.multiple_of(b * count, count), count)
            back[c, at] = lines.reshape(count, slots, GROUP, nz)
            return carry

        lax.fori_loop(0, span_rows // step, body, 0)
        each_peer(lambda peer: back_copy(c, peer, me).start())
        target[me, c] = back[c, me]

    def denoise(outer, index, spans):
        dual_x, dual_y, dual_z = duals[3 * index : 3 * index + 3]
        members = [(g, low <= g < high) for low, high in spans for g in range(low - 1, high + 1)]
        wide = len(members) * GROUP
        lane = lax.broadcasted_iota(jnp.int32, (wide, LANES), 1)
        is_first, is_last = lane == 0, lane == LANES - 1
        nothing = jnp.zeros((wide, LANES), f32)
        edge = members[0][0] < 0
        if edge:
            place = lax.broadcasted_iota(jnp.int32, (GROUP, nz), 0) * 0 + me
            inside = jnp.concatenate(
                [
                    jnp.where(place > 0, 1.0, 0.0)
                    if g < 0
                    else jnp.where(place < n - 1, 1.0, 0.0)
                    if g >= groups
                    else jnp.ones((GROUP, nz), f32)
                    for g, _ in members
                ],
                axis=0,
            )

        def sum_x(value):
            return pltpu.roll(value, 1, 0) + pltpu.roll(value, wide - 1, 0)

        def sum_z(value):
            pieces = [value[:, z : z + LANES] for z in range(0, nz, LANES)]
            ups = [nothing] + [pltpu.roll(piece, 1, 1) for piece in pieces]
            downs = [pltpu.roll(piece, LANES - 1, 1) for piece in pieces] + [nothing]
            return jnp.concatenate(
                [
                    jnp.where(is_first, ups[z], ups[z + 1])
                    + jnp.where(is_last, downs[z + 1], downs[z])
                    for z in range(len(pieces))
                ],
                axis=1,
            )

        def collect(y, carry):
            pieces = []
            for g, _ in members:
                if g < 0:
                    pieces.append(halo[0, y])
                elif g >= groups:
                    pieces.append(halo[1, y])
                else:
                    pieces.append(target[y, seat[g][0], seat[g][1]])
            goal[y + 1, 0:wide, :] = jnp.concatenate(pieces, axis=0)
            return carry

        lax.fori_loop(0, ny, collect, 0)
        for sweep in range(PASSES):
            origin = goal if sweep == 0 else lead
            fresh = outer == 0 and sweep == 0

            def rise(y):
                here = origin[y, 0:wide, :]
                twice = here + here
                raised = [
                    sum_x(here) - twice,
                    origin[y - 1, 0:wide, :] + origin[y + 1, 0:wide, :] - twice,
                    sum_z(here) - twice,
                ]
                if not fresh:
                    raised = [
                        dual[y] + bend for dual, bend in zip((dual_x, dual_y, dual_z), raised)
                    ]
                norm = raised[0] * raised[0] + raised[1] * raised[1] + raised[2] * raised[2]
                shrink = lax.rsqrt(
                    jnp.maximum(1.0 / relax**2, norm * (1.0 / (bound_dual * relax) ** 2))
                )
                if edge:
                    shrink = shrink * inside
                dual_x[y] = raised[0] * shrink
                dual_y[y] = raised[1] * shrink
                dual_z[y] = raised[2] * shrink

            def fall(y):
                in_x, in_y, in_z = dual_x[y], dual_y[y], dual_z[y]
                middle = in_x + in_y + in_z
                adjoint = (
                    sum_x(in_x) + (dual_y[y - 1] + dual_y[y + 1]) + sum_z(in_z) - (middle + middle)
                ) * (step_primal * step_dual / (1.0 + step_primal))
                if sweep == 0:
                    old = goal[y, 0:wide, :]
                    updated = old - adjoint
                else:
                    old = field[y, 0:wide, :]
                    updated = (
                        old * (1.0 / (1.0 + step_primal))
                        + goal[y, 0:wide, :] * (step_primal / (1.0 + step_primal))
                        - adjoint
                    )
                if sweep < PASSES - 1:
                    if edge:
                        updated = updated * inside
                    lead[y, 0:wide, :] = updated + updated - old
                    field[y, 0:wide, :] = updated
                    return
                for i, (g, own) in enumerate(members):
                    if own:
                        lines = updated[i * GROUP : (i + 1) * GROUP, :]
                        if outer < OUTER - 1:
                            current[y - 1, seat[g][0], seat[g][1]] = lines
                        else:
                            out_ref[y - 1, g * GROUP : (g + 1) * GROUP, :] = lines * (1.0 / gain)

            rise(1)

            def body(y, carry):
                rise(y)
                fall(y - 1)
                return carry

            lax.fori_loop(2, ny + 1, body, 0)
            fall(ny)

    lax.fori_loop(0, ny, stage, 0)
    pl.semaphore_wait(barrier, n - 1)
    for c in range(chunks):
        send_forward(c)

    @pl.when(me == 0)
    def _():
        halo[0] = jnp.zeros(halo.shape[1:], f32)

    @pl.when(me == n - 1)
    def _():
        halo[1] = jnp.zeros(halo.shape[1:], f32)

    for ref in [goal, lead] + list(duals[1::3]):
        ref[0] = jnp.zeros(ref.shape[1:], f32)
        ref[ny + 1] = jnp.zeros(ref.shape[1:], f32)
    make_tables()
    make_filter()
    quarter = groups // 4
    for outer in range(OUTER):
        filtered(outer)
        for c in range(chunks):
            every_other(lambda peer: forward_copy(c, peer, me).wait_send())
        for c in range(chunks):
            send_back(c)

        def arrive(some):
            for c in some:
                every_other(lambda owner: back_copy(c, owner, owner).wait_recv())

        arrive([0])

        @pl.when(me < n - 1)
        def _():
            halo_copy(0).start()

        @pl.when(me > 0)
        def _():
            halo_copy(1).start()

        early = list(range(1, quarter + 1)) if chunks > 1 else []
        arrive(early)

        @pl.when(me > 0)
        def _():
            halo_copy(0).wait_recv()

        @pl.when(me < n - 1)
        def _():
            halo_copy(1).wait_recv()

        done = 0
        if chunks > 1:
            denoise(outer, 0, [(0, quarter), (groups - quarter, groups)])
            done = quarter
            if outer < OUTER - 1:
                for c in range(done):
                    send_forward(c)
            arrive(range(quarter + 1, chunks))
            denoise(outer, 1, [(quarter, groups - quarter)])
        else:
            denoise(outer, 0, [(0, groups)])

        @pl.when(me < n - 1)
        def _():
            halo_copy(0).wait_send()

        @pl.when(me > 0)
        def _():
            halo_copy(1).wait_send()

        for c in range(chunks):
            every_other(lambda peer: back_copy(c, peer, me).wait_send())
        if outer < OUTER - 1:
            for c in range(done, chunks):
                send_forward(c)


def constants(n, rows, order, nz):
    nx = n * rows
    place = np.array(
        [
            d * rows + g * GROUP + r
            for some in order
            for d in range(n)
            for g in some
            for r in range(GROUP)
        ]
    )
    turn = 2.0 * math.pi / nx
    coarse = (place[::GROUP, None] * place[None, :] % nx) * turn
    fine = (np.arange(GROUP)[:, None] * place[None, :] % nx) * turn
    norm = 1.0 / math.sqrt(nx)
    tables = (
        np.cos(coarse),
        np.sin(coarse),
        (np.cos(fine) + np.sin(fine)) * norm,
        (np.cos(fine) - np.sin(fine)) * norm,
    )
    k = np.arange(nz)
    angle = (k[:, None] * k[None, :] % nz) * (2.0 * math.pi / nz)
    cas_z = ((np.cos(angle) + np.sin(angle)) / math.sqrt(nz)).astype(np.float32)
    z_high = cas_z.astype(bf16)
    z_low = (cas_z - z_high.astype(np.float32)).astype(bf16)
    return [jnp.asarray(t, f32) for t in tables] + [jnp.asarray(z_high), jnp.asarray(z_low)]


def local(n, observed, tf_table, tilt_index, wedge):
    rows, ny, nz = observed.shape
    nx = n * rows
    groups = rows // GROUP
    if groups % 4 == 0:
        order = [(c, groups - 1 - c) for c in range(groups // 2)]
        sizes = [groups // 2 + 4, groups // 2 + 2]
    else:
        order = [tuple(range(groups))]
        sizes = [groups + 2]
    chunks, slots = len(order), len(order[0])
    lines, columns = tilt_index.shape
    depth, width = -(-lines // 128) * 128, -(-columns // 128) * 128
    tables = constants(n, rows, order, nz)
    tiles = observed.reshape(rows, ny // GROUP, GROUP, nz // LANES, LANES)
    tiles = tiles.transpose(0, 1, 3, 2, 4).reshape(-1, LANES)
    vmem = pl.BlockSpec(memory_space=pltpu.VMEM)
    smem = pl.BlockSpec(memory_space=pltpu.SMEM)
    tile_rows = [size * GROUP for size in sizes]
    scratch_tile = pltpu.VMEM((ny + 2, max(tile_rows), nz), f32)
    plane = pltpu.VMEM((nx, nz), f32)
    blocks = pltpu.VMEM((chunks, n, slots, GROUP, nz), f32)
    cells = pltpu.VMEM((ny, chunks, slots, GROUP, nz), f32)
    semaphores = pltpu.SemaphoreType.DMA((chunks, n))
    result = pl.pallas_call(
        functools.partial(kernel, n, rows, order),
        out_shape=jax.ShapeDtypeStruct((ny, rows, nz), f32),
        in_specs=[vmem, smem] + [vmem] * 8,
        out_specs=vmem,
        scratch_shapes=[
            blocks,
            plane,
            plane,
            plane,
            pltpu.VMEM((nx, nx), bf16),
            pltpu.VMEM((nx, nx), bf16),
            pltpu.VMEM((nx, nz), bf16),
            pltpu.VMEM((nx, nz), bf16),
            blocks,
            cells,
            pltpu.VMEM((2, ny, GROUP, nz), f32),
            scratch_tile,
            scratch_tile,
            scratch_tile,
            [pltpu.VMEM((ny + 2, size, nz), f32) for size in tile_rows for _ in range(3)],
            cells,
            pltpu.VMEM((width, depth), f32),
            semaphores,
            semaphores,
            semaphores,
            semaphores,
            pltpu.SemaphoreType.DMA((2,)),
            pltpu.SemaphoreType.DMA((2,)),
        ],
        compiler_params=pltpu.CompilerParams(
            collective_id=0, has_side_effects=True, vmem_limit_bytes=60 * 1024 * 1024
        ),
    )(tiles, tf_table, tilt_index.T, wedge.T, *tables)
    return jnp.swapaxes(result, 0, 1)


def solution(mesh):
    in_specs = (P(("groups", "gy"), None, None), P(), P(), P())
    out_specs = P(("groups", "gy"), None, None)
    body = functools.partial(local, mesh.shape["gy"])
    return jax.shard_map(body, mesh=mesh, in_specs=in_specs, out_specs=out_specs, check_vma=False)
```

```python
import functools
import math

import jax
import jax.numpy as jnp
import numpy as np
from jax import lax
from jax.experimental import pallas as pl
from jax.experimental.pallas import tpu as pltpu
from jax.sharding import PartitionSpec as P

OUTER = 2
PASSES = 2
GROUP = 8
LANES = 128
STEP = 2

step_dual = 0.14
step_primal = 0.14
huber_eps = 0.05
bound_dual = 0.5
relax = 1.0 / (1.0 + step_dual * huber_eps / bound_dual)
gain = step_dual * relax
MESH = pl.DeviceIdType.MESH
f32 = jnp.float32
bf16 = jnp.bfloat16


def split(value):
    high = value.astype(bf16)
    low = (value - high.astype(f32)).astype(bf16)
    return high, low


def dot3(a_high, a_low, b_high, b_low):
    dot = functools.partial(jnp.dot, preferred_element_type=f32)
    return dot(a_high, b_high) + (dot(a_high, b_low) + dot(a_low, b_high))


def kernel(
    n, rows, order,
    cells_ref, table_ref, tilt_ref, wedge_ref, cos_ref, sin_ref, cas_ref, case_ref, zh_ref, zl_ref,
    out_ref,
    gathered, total, data_term, prior_gain, x_high, x_low, m_high, m_low, back,
    target, halo, goal, field, lead, duals, current, code,
    send_sem, recv_sem, back_send, back_recv, halo_send, halo_recv,
):
    me = lax.axis_index("gy")
    chunks, slots = len(order), len(order[0])
    groups = chunks * slots
    seat = {g: (c, s) for c in range(chunks) for s, g in enumerate(order[c])}
    part = slots * GROUP
    ny, nz = out_ref.shape[0], out_ref.shape[2]
    nx = n * rows
    half = n // 2
    span_rows = n * part
    block = math.gcd(nx, 256)
    row_blocks = nx // block

    barrier = pltpu.get_barrier_semaphore()

    def greet(o, carry):
        pl.semaphore_signal(
            barrier, inc=1, device_id={"gy": lax.rem(me + o, n)}, device_id_type=MESH
        )
        return carry

    lax.fori_loop(1, n, greet, 0)

    def each_peer(action):
        def first(k, carry):
            action((1 - me // half) * half + lax.rem(me + k, half))
            return carry

        def second(k, carry):
            action((me // half) * half + lax.rem(me + k, half))
            return carry

        lax.fori_loop(0, half, first, 0)
        lax.fori_loop(1, half, second, 0)

    def every_other(action):
        def step(o, carry):
            action(lax.rem(me + o, n))
            return carry

        lax.fori_loop(1, n, step, 0)

    def forward_copy(c, peer, owner):
        return pltpu.make_async_remote_copy(
            src_ref=current.at[peer, c],
            dst_ref=gathered.at[c, owner],
            send_sem=send_sem.at[c, peer],
            recv_sem=recv_sem.at[c, owner],
            device_id={"gy": peer},
            device_id_type=MESH,
        )

    def back_copy(c, peer, owner):
        return pltpu.make_async_remote_copy(
            src_ref=back.at[c, peer],
            dst_ref=target.at[owner, c],
            send_sem=back_send.at[c, peer],
            recv_sem=back_recv.at[c, owner],
            device_id={"gy": peer},
            device_id_type=MESH,
        )

    def halo_copy(side):
        return pltpu.make_async_remote_copy(
            src_ref=target.at[:, 0, slots - 1 if side == 0 else 0],
            dst_ref=halo.at[side],
            send_sem=halo_send.at[side],
            recv_sem=halo_recv.at[side],
            device_id={"gy": lax.rem(me + (1 if side == 0 else n - 1), n)},
            device_id_type=MESH,
        )

    def send_forward(c):
        each_peer(lambda peer: forward_copy(c, peer, me).start())
        gathered[c, me] = current[me, c]

    def stage(y, carry):
        stride = ny * nz // LANES
        for z in range(nz // LANES):
            first = (y // GROUP * (nz // LANES) + z) * GROUP + y % GROUP
            lines = cells_ref[pl.ds(first, rows, stride=stride), :]
            for g, (c, s) in seat.items():
                current[y, c, s, :, z * LANES : (z + 1) * LANES] = lines[
                    g * GROUP : (g + 1) * GROUP, :
                ]
        return carry

    def make_tables():
        def body(m, carry):
            lines = jnp.concatenate(
                [
                    cos_ref[pl.ds(k, 1), :] * cas_ref[...] + sin_ref[pl.ds(k, 1), :] * case_ref[...]
                    for k in (2 * m, 2 * m + 1)
                ],
                axis=0,
            )
            at = pl.ds(pl.multiple_of(m * 2 * GROUP, 2 * GROUP), 2 * GROUP)
            x_high[at, :], x_low[at, :] = split(lines)
            return carry

        lax.fori_loop(0, nx // (2 * GROUP), body, 0)

    def make_filter():
        columns, lines = tilt_ref.shape
        code[...] = jnp.zeros_like(code)
        code[0:columns, 0:lines] = jnp.where(wedge_ref[...] == 0, 0, tilt_ref[...] + 1).astype(f32)
        width, depth = code.shape
        kz = lax.broadcasted_iota(jnp.int32, (nz, width), 0)
        pick_z = jnp.where(
            lax.broadcasted_iota(jnp.int32, (nz, width), 1) == jnp.minimum(kz, nz - kz), 1.0, 0.0
        ).astype(bf16)
        spread = jnp.dot(pick_z, code[...].astype(bf16), preferred_element_type=f32).astype(bf16)

        def body(b, carry):
            line = b * block + lax.broadcasted_iota(jnp.int32, (block, depth), 0)
            c = line // span_rows
            slot = line % part // GROUP
            group = slot if chunks == 1 else jnp.where(slot == 0, c, groups - 1 - c)
            kx = line % span_rows // part * rows + group * GROUP + line % GROUP
            column = lax.broadcasted_iota(jnp.int32, (block, depth), 1)
            pick_x = jnp.where(column == jnp.minimum(kx, nx - kx), 1.0, 0.0).astype(bf16)
            which = lax.dot_general(
                pick_x, spread, (((1,), (1,)), ((), ())), preferred_element_type=f32
            )
            response = jnp.zeros_like(which)
            for level in range(table_ref.shape[0]):
                response = jnp.where(which == level + 1.0, table_ref[level], response)
            prior = 1.0 / (response * response + 1.0)
            at = pl.ds(pl.multiple_of(b * block, block), block)
            prior_gain[at, :] = prior
            data_term[at, :] = response * prior
            return carry

        lax.fori_loop(0, row_blocks, body, 0)

    def filtered(outer):
        for c in range(chunks):
            every_other(lambda owner: forward_copy(c, owner, owner).wait_recv())
            high, low = split(gathered[c].reshape(span_rows, nz))
            high, low = split(dot3(high, low, zh_ref[...], zl_ref[...]))

            def body(b, carry):
                at = pl.ds(pl.multiple_of(b * block, block), block)
                span = pl.ds(c * span_rows, span_rows)
                spectrum = dot3(x_high[at, span], x_low[at, span], high, low)
                if c > 0:
                    spectrum = total[at, :] + spectrum
                if c < chunks - 1:
                    total[at, :] = spectrum
                    return carry
                if outer == 0:
                    spectrum = spectrum * gain
                    data_term[at, :] = data_term[at, :] * spectrum
                a_high, a_low = split(data_term[at, :] + prior_gain[at, :] * spectrum)
                m_high[at, :], m_low[at, :] = split(dot3(a_high, a_low, zh_ref[...], zl_ref[...]))
                return carry

            lax.fori_loop(0, row_blocks, body, 0)

    def send_back(c):
        step = math.gcd(span_rows, 256)

        def body(b, carry):
            line = pl.ds(pl.multiple_of(c * span_rows + b * step, step), step)
            lines = dot3(x_high[line, :], x_low[line, :], m_high[...], m_low[...])
            count = step // part
            at = pl.ds(pl.multiple_of(b * count, count), count)
            back[c, at] = lines.reshape(count, slots, GROUP, nz)
            return carry

        lax.fori_loop(0, span_rows // step, body, 0)
        each_peer(lambda peer: back_copy(c, peer, me).start())
        target[me, c] = back[c, me]

    def denoise(outer, index, spans):
        dual_x, dual_y, dual_z = duals[3 * index : 3 * index + 3]
        members = [(g, low <= g < high) for low, high in spans for g in range(low - 1, high + 1)]
        wide = len(members) * GROUP
        step = STEP * GROUP
        strips = [(r, min(r + step, wide)) for r in range(0, wide, step)]
        edge = members[0][0] < 0
        if edge:
            place = lax.broadcasted_iota(jnp.int32, (GROUP, nz), 0) * 0 + me
            inside = jnp.concatenate(
                [
                    jnp.where(place > 0, 1.0, 0.0)
                    if g < 0
                    else jnp.where(place < n - 1, 1.0, 0.0)
                    if g >= groups
                    else jnp.ones((GROUP, nz), f32)
                    for g, _ in members
                ],
                axis=0,
            )

        def sum_x(ref, y, start, stop):
            first, last = max(start - GROUP, 0), min(stop + GROUP, wide)
            value = ref[y, first:last, :]
            both = pltpu.roll(value, 1, 0) + pltpu.roll(value, last - first - 1, 0)
            return both[start - first : stop - first, :]

        def sum_z(value):
            pieces = [value[:, z : z + LANES] for z in range(0, nz, LANES)]
            nothing = jnp.zeros_like(pieces[0])
            lane = lax.broadcasted_iota(jnp.int32, pieces[0].shape, 1)
            ups = [nothing] + [pltpu.roll(piece, 1, 1) for piece in pieces]
            downs = [pltpu.roll(piece, LANES - 1, 1) for piece in pieces] + [nothing]
            return jnp.concatenate(
                [
                    jnp.where(lane == 0, ups[z], ups[z + 1])
                    + jnp.where(lane == LANES - 1, downs[z + 1], downs[z])
                    for z in range(len(pieces))
                ],
                axis=1,
            )

        def at_edge(start, stop):
            some = [g for g, _ in members[start // GROUP : stop // GROUP]]
            return min(some) < 0 or max(some) >= groups

        def collect(y, carry):
            pieces = []
            for g, _ in members:
                if g < 0:
                    pieces.append(halo[0, y])
                elif g >= groups:
                    pieces.append(halo[1, y])
                else:
                    pieces.append(target[y, seat[g][0], seat[g][1]])
            goal[y + 1, 0:wide, :] = jnp.concatenate(pieces, axis=0)
            return carry

        lax.fori_loop(0, ny, collect, 0)
        for sweep in range(PASSES):
            origin = goal if sweep == 0 else lead
            fresh = outer == 0 and sweep == 0

            def rise(y):
                for start, stop in strips:
                    here = origin[y, start:stop, :]
                    twice = here + here
                    raised = [
                        sum_x(origin, y, start, stop) - twice,
                        origin[y - 1, start:stop, :] + origin[y + 1, start:stop, :] - twice,
                        sum_z(here) - twice,
                    ]
                    if not fresh:
                        raised = [
                            dual[y, start:stop, :] + bend
                            for dual, bend in zip((dual_x, dual_y, dual_z), raised)
                        ]
                    norm = raised[0] * raised[0] + raised[1] * raised[1] + raised[2] * raised[2]
                    shrink = lax.rsqrt(
                        jnp.maximum(1.0 / relax**2, norm * (1.0 / (bound_dual * relax) ** 2))
                    )
                    if at_edge(start, stop):
                        shrink = shrink * inside[start:stop, :]
                    dual_x[y, start:stop, :] = raised[0] * shrink
                    dual_y[y, start:stop, :] = raised[1] * shrink
                    dual_z[y, start:stop, :] = raised[2] * shrink

            def fall(y):
                for start, stop in strips:
                    in_x, in_y, in_z = [
                        dual[y, start:stop, :] for dual in (dual_x, dual_y, dual_z)
                    ]
                    middle = in_x + in_y + in_z
                    adjoint = (
                        sum_x(dual_x, y, start, stop)
                        + (dual_y[y - 1, start:stop, :] + dual_y[y + 1, start:stop, :])
                        + sum_z(in_z)
                        - (middle + middle)
                    ) * (step_primal * step_dual / (1.0 + step_primal))
                    if sweep == 0:
                        old = goal[y, start:stop, :]
                        updated = old - adjoint
                    else:
                        old = field[y, start:stop, :]
                        updated = (
                            old * (1.0 / (1.0 + step_primal))
                            + goal[y, start:stop, :] * (step_primal / (1.0 + step_primal))
                            - adjoint
                        )
                    if sweep < PASSES - 1:
                        if at_edge(start, stop):
                            updated = updated * inside[start:stop, :]
                        lead[y, start:stop, :] = updated + updated - old
                        field[y, start:stop, :] = updated
                        continue
                    for i, (g, own) in enumerate(members):
                        if own and start <= i * GROUP < stop:
                            lines = updated[i * GROUP - start : (i + 1) * GROUP - start, :]
                            if outer < OUTER - 1:
                                current[y - 1, seat[g][0], seat[g][1]] = lines
                            else:
                                out_ref[y - 1, g * GROUP : (g + 1) * GROUP, :] = lines * (1.0 / gain)

            rise(1)

            def body(y, carry):
                rise(y)
                fall(y - 1)
                return carry

            lax.fori_loop(2, ny + 1, body, 0)
            fall(ny)

    lax.fori_loop(0, ny, stage, 0)
    pl.semaphore_wait(barrier, n - 1)
    for c in range(chunks):
        send_forward(c)

    @pl.when(me == 0)
    def _():
        halo[0] = jnp.zeros(halo.shape[1:], f32)

    @pl.when(me == n - 1)
    def _():
        halo[1] = jnp.zeros(halo.shape[1:], f32)

    for ref in [goal, lead] + list(duals[1::3]):
        ref[0] = jnp.zeros(ref.shape[1:], f32)
        ref[ny + 1] = jnp.zeros(ref.shape[1:], f32)
    make_tables()
    make_filter()
    quarter = groups // 4
    for outer in range(OUTER):
        filtered(outer)
        for c in range(chunks):
            every_other(lambda peer: forward_copy(c, peer, me).wait_send())
        for c in range(chunks):
            send_back(c)

        def arrive(some):
            for c in some:
                every_other(lambda owner: back_copy(c, owner, owner).wait_recv())

        arrive([0])

        @pl.when(me < n - 1)
        def _():
            halo_copy(0).start()

        @pl.when(me > 0)
        def _():
            halo_copy(1).start()

        early = list(range(1, quarter + 1)) if chunks > 1 else []
        arrive(early)

        @pl.when(me > 0)
        def _():
            halo_copy(0).wait_recv()

        @pl.when(me < n - 1)
        def _():
            halo_copy(1).wait_recv()

        done = 0
        if chunks > 1:
            done = quarter
            arrive(range(quarter + 1, chunks))
            denoise(outer, 0, [(0, groups)])
            done = 0
        else:
            denoise(outer, 0, [(0, groups)])

        @pl.when(me < n - 1)
        def _():
            halo_copy(0).wait_send()

        @pl.when(me > 0)
        def _():
            halo_copy(1).wait_send()

        for c in range(chunks):
            every_other(lambda peer: back_copy(c, peer, me).wait_send())
        if outer < OUTER - 1:
            for c in range(done, chunks):
                send_forward(c)


def constants(n, rows, order, nz):
    nx = n * rows
    place = np.array(
        [
            d * rows + g * GROUP + r
            for some in order
            for d in range(n)
            for g in some
            for r in range(GROUP)
        ]
    )
    turn = 2.0 * math.pi / nx
    coarse = (place[::GROUP, None] * place[None, :] % nx) * turn
    fine = (np.arange(GROUP)[:, None] * place[None, :] % nx) * turn
    norm = 1.0 / math.sqrt(nx)
    tables = (
        np.cos(coarse),
        np.sin(coarse),
        (np.cos(fine) + np.sin(fine)) * norm,
        (np.cos(fine) - np.sin(fine)) * norm,
    )
    k = np.arange(nz)
    angle = (k[:, None] * k[None, :] % nz) * (2.0 * math.pi / nz)
    cas_z = ((np.cos(angle) + np.sin(angle)) / math.sqrt(nz)).astype(np.float32)
    z_high = cas_z.astype(bf16)
    z_low = (cas_z - z_high.astype(np.float32)).astype(bf16)
    return [jnp.asarray(t, f32) for t in tables] + [jnp.asarray(z_high), jnp.asarray(z_low)]


def local(n, observed, tf_table, tilt_index, wedge):
    rows, ny, nz = observed.shape
    nx = n * rows
    groups = rows // GROUP
    if groups % 4 == 0:
        order = [(c, groups - 1 - c) for c in range(groups // 2)]
        sizes = [groups + 2]
    else:
        order = [tuple(range(groups))]
        sizes = [groups + 2]
    chunks, slots = len(order), len(order[0])
    lines, columns = tilt_index.shape
    depth, width = -(-lines // 128) * 128, -(-columns // 128) * 128
    tables = constants(n, rows, order, nz)
    tiles = observed.reshape(rows, ny // GROUP, GROUP, nz // LANES, LANES)
    tiles = tiles.transpose(0, 1, 3, 2, 4).reshape(-1, LANES)
    vmem = pl.BlockSpec(memory_space=pltpu.VMEM)
    smem = pl.BlockSpec(memory_space=pltpu.SMEM)
    tile_rows = [size * GROUP for size in sizes]
    scratch_tile = pltpu.VMEM((ny + 2, max(tile_rows), nz), f32)
    plane = pltpu.VMEM((nx, nz), f32)
    blocks = pltpu.VMEM((chunks, n, slots, GROUP, nz), f32)
    cells = pltpu.VMEM((ny, chunks, slots, GROUP, nz), f32)
    semaphores = pltpu.SemaphoreType.DMA((chunks, n))
    result = pl.pallas_call(
        functools.partial(kernel, n, rows, order),
        out_shape=jax.ShapeDtypeStruct((ny, rows, nz), f32),
        in_specs=[vmem, smem] + [vmem] * 8,
        out_specs=vmem,
        scratch_shapes=[
            blocks,
            plane,
            plane,
            plane,
            pltpu.VMEM((nx, nx), bf16),
            pltpu.VMEM((nx, nx), bf16),
            pltpu.VMEM((nx, nz), bf16),
            pltpu.VMEM((nx, nz), bf16),
            blocks,
            cells,
            pltpu.VMEM((2, ny, GROUP, nz), f32),
            scratch_tile,
            scratch_tile,
            scratch_tile,
            [pltpu.VMEM((ny + 2, size, nz), f32) for size in tile_rows for _ in range(3)],
            cells,
            pltpu.VMEM((width, depth), f32),
            semaphores,
            semaphores,
            semaphores,
            semaphores,
            pltpu.SemaphoreType.DMA((2,)),
            pltpu.SemaphoreType.DMA((2,)),
        ],
        compiler_params=pltpu.CompilerParams(
            collective_id=0, has_side_effects=True, vmem_limit_bytes=60 * 1024 * 1024
        ),
    )(tiles, tf_table, tilt_index.T, wedge.T, *tables)
    return jnp.swapaxes(result, 0, 1)


def solution(mesh):
    in_specs = (P(("groups", "gy"), None, None), P(), P(), P())
    out_specs = P(("groups", "gy"), None, None)
    body = functools.partial(local, mesh.shape["gy"])
    return jax.shard_map(body, mesh=mesh, in_specs=in_specs, out_specs=out_specs, check_vma=False)
```
